768 devices in a mesh: section: 24 (over z, x_lo), tower: 2 (over x_hi), lane: 16 (over y, core).
Axes of the slice: x: 4 (x_hi: 2, x_lo: 2; x = x_hi * 2 + x_lo), y: 8, z: 12, core: 2. Of those that a mesh axis runs over, the one named last changes fastest.
Arguments:
- in_flight: bfloat16 [24, 2, 256, 3072], P('section', 'tower', 'lane'), may hold values from -6 to 6
- fresh_batches: bfloat16 [16, 2, 256, 3072], P(None, 'tower', 'lane'), may hold values from -6 to 6
- offsets: int32 [16], P('lane'), may hold values from 0 to 15, as said below
- norm_gain: float32 [24, 2, 3072], P('section', 'tower'), may hold values from 0.5 to 3
- w_query: bfloat16 [24, 2, 3072, 2048], P('section', 'tower', None, 'lane'), may hold values from -0.109375 to 0.109375
- w_keyval: bfloat16 [24, 2, 2, 3072, 2048], P('section', 'tower', None, None, 'lane'), may hold values from -0.109375 to 0.109375
- w_out: bfloat16 [24, 2, 2048, 3072], P('section', 'tower', 'lane'), may hold values from -0.125 to 0.125
Outputs:
- states: bfloat16 [2, 24, 2, 256, 3072], P(None, 'section', 'tower', 'lane')
The draws below stay inside these ranges and needn't reach their ends.
Inputs may be any that keep to these rules, and one draw needn't show every extreme that they name: offsets is a permutation of 0 to 15.
All inputs are finite; a program needn't handle non-finite values.
Results may differ from the reference program's by a relative error of at most 0.017.
Values may be sent and summed in bfloat16 or wider, within the bound.
A program may use at most 32 MiB of HBM per device.

```python
import jax
import jax.numpy as jnp
from jax import lax

D = 3072
HEAD_DIM = 128
HEADS = 16
TOK = 16
NF = 16
ROWS = 256
N_SECTION = 24
N_LANE = 16


def draw_offsets(key, part):
    return jax.random.permutation(key, N_LANE).astype(jnp.int32)


def draw_norm_gain(key, part):
    low, high = (jnp.log(0.5), jnp.log(2.0))
    uniform_draw = jax.random.uniform(key, (N_SECTION, 2, D), jnp.float32, low, high)
    return jnp.exp(uniform_draw).astype(jnp.float32)


def block_levels(stream_key, dims, split, low, high):
    def one(position, blocks):
        heights = jax.random.uniform(jax.random.fold_in(jax.random.fold_in(stream_key, 6), position), (blocks,), jnp.float32, low / len(split), high / len(split))
        return jnp.repeat(jnp.exp(heights), dims[position] // blocks).reshape((-1,) + (1,) * (len(dims) - position - 1))

    factor_of = one(*split[0])
    for cut in split[1:]:
        factor_of = factor_of * one(*cut)
    return factor_of


def centred(stream_key, extent, width, most, cuts=(), held_as=jnp.bfloat16):
    result = width * jax.random.normal(stream_key, extent, jnp.float32)
    if cuts:
        result = result * block_levels(stream_key, extent, cuts, -0.22, 0.18)
    return jnp.clip(result, -most, most).astype(held_as)


def setup_inputs(seed: int = 0) -> dict:
    key_list = jax.random.split(jax.random.key(seed), 8)
    in_flight = centred(key_list[0], (N_SECTION, 2, ROWS, D), 1.0, 6.0, ((0, 24), (1, 2), (2, 16)))
    fresh_batches = centred(key_list[1], (NF, 2, ROWS, D), 1.0, 6.0, ((1, 2), (2, 16)))
    offsets = draw_offsets(jax.random.fold_in(key_list[7], 71), 0)
    norm_gain = draw_norm_gain(jax.random.fold_in(key_list[7], 71), 0)
    w_query = centred(key_list[4], (N_SECTION, 2, D, HEADS * HEAD_DIM), D ** -0.5, 0.109375, ((0, 24), (1, 2), (3, 16)))
    w_keyval = centred(key_list[5], (N_SECTION, 2, 2, D, HEADS * HEAD_DIM), D ** -0.5, 0.109375, ((0, 24), (1, 2), (4, 16)))
    w_out = centred(key_list[6], (N_SECTION, 2, HEADS * HEAD_DIM, D), (HEADS * HEAD_DIM) ** -0.5, 0.125, ((0, 24), (1, 2), (2, 16)))
    return {"in_flight": in_flight, "fresh_batches": fresh_batches, "offsets": offsets, "norm_gain": norm_gain, "w_query": w_query, "w_keyval": w_keyval, "w_out": w_out}


epsilon = 1e-06

def section_layer(packed):
    state, norm_w, wq_section, wkv_section, wo_section = packed
    wide = state.astype(jnp.float32)
    normed = (wide * lax.rsqrt(lax.optimization_barrier(jnp.mean(wide * wide, -1, keepdims=True)) + epsilon) * norm_w[:, None, :]).astype(jnp.bfloat16)
    partner = normed[::-1]
    query = jnp.einsum('trd,tdh->trh', normed.astype(jnp.float32), wq_section.astype(jnp.float32)).astype(jnp.bfloat16)
    keys = jnp.einsum('trd,tdh->trh', partner.astype(jnp.float32), wkv_section[:, 0].astype(jnp.float32)).astype(jnp.bfloat16)
    values = jnp.einsum('trd,tdh->trh', partner.astype(jnp.float32), wkv_section[:, 1].astype(jnp.float32)).astype(jnp.bfloat16)
    shaped = (2, N_LANE, TOK, HEADS, HEAD_DIM)
    scores = jnp.einsum('tlqhe,tlkhe->tlhqk', query.reshape(shaped).astype(jnp.float32), keys.reshape(shaped).astype(jnp.float32)) / jnp.sqrt(jnp.float32(HEAD_DIM))
    attn_weights = jax.nn.softmax(scores, axis=-1).astype(jnp.bfloat16)
    mixed = jnp.einsum('tlhqk,tlkhe->tlqhe', attn_weights.astype(jnp.float32), values.reshape(shaped).astype(jnp.float32)).astype(jnp.bfloat16)
    head_cols = HEADS // N_LANE * HEAD_DIM
    mixed = mixed.reshape(2, ROWS, N_LANE, head_cols)
    wo_groups = wo_section.reshape(2, N_LANE, head_cols, D)
    parts = jnp.einsum('trgc,tgcd->tgrd', mixed.astype(jnp.float32), wo_groups.astype(jnp.float32))
    head_total = lax.optimization_barrier(jnp.sum(parts, axis=1))
    return (wide + head_total).astype(jnp.bfloat16)

def reference(in_flight, fresh_batches, offsets, norm_gain, w_query, w_keyval, w_out):
    first = lax.map(section_layer, (in_flight, norm_gain, w_query, w_keyval, w_out))
    shaped_fresh = fresh_batches.reshape(NF, 2, N_LANE, TOK, D)
    picked = shaped_fresh[offsets.astype(jnp.int32), :, jnp.arange(N_LANE, dtype=jnp.int32)]
    picked = jnp.transpose(picked, (1, 0, 2, 3)).reshape(2, ROWS, D)
    second_in = jnp.concatenate([picked[None], first[:-1]], axis=0)
    second = lax.map(section_layer, (second_in, norm_gain, w_query, w_keyval, w_out))
    return jnp.stack([first, second])
```

```python
import functools
import math

import jax
import jax.numpy as jnp
from jax import lax
from jax.experimental import pallas as pl
from jax.experimental.pallas import tpu as pltpu
from jax.sharding import PartitionSpec as P

HEAD = 128
EPS = 1e-06
MESH = pl.DeviceIdType.MESH
BF = jnp.bfloat16
F32 = jnp.float32
STAGES = ((0, 1), (1, 3), (3, 5), (5, 7), (7, 8))
BACK = (0, 1, 3, 5, 7)
AHEAD = (0, 2, 4, 6, 7)


def normed(rows, gain):
    wide = rows.astype(F32)
    mean = jnp.mean(wide * wide, -1, keepdims=True)
    return (wide * lax.rsqrt(mean + EPS) * gain).astype(BF)


def kernel(
    n_sec,
    n_lane,
    x_ref,
    fresh_ref,
    off_ref,
    gain_ref,
    wq_ref,
    wkv_ref,
    wo_ref,
    out_ref,
    xo,
    xp,
    gains,
    w_all,
    wo_all,
    fresh,
    rows,
    part,
    rsend,
    rrecv,
    outv,
    ag_s,
    ag_r,
    rs_s,
    rs_r,
    in_s,
    in_r,
    w_s,
    w_r,
    load,
):
    section = lax.axis_index("section")
    tower = lax.axis_index("tower")
    lane = lax.axis_index("lane")
    d = x_ref.shape[-1]
    hd = d // 2
    tok = x_ref.shape[0]
    up = {"lane": lax.rem(lane + 2, n_lane)}
    down = {"lane": lax.rem(lane + n_lane - 2, n_lane)}
    mate = {"lane": lane + 1 - 2 * lax.rem(lane, 2)}
    other = {"tower": 1 - tower}
    later = lax.rem(section + 1, n_sec)
    sooner = lax.rem(section + n_sec - 1, n_sec)

    loads = [
        (x_ref, xo.at[0]),
        (gain_ref, gains.at[0]),
        (wq_ref, w_all.at[:, pl.ds(0, HEAD)]),
        (wkv_ref.at[0], w_all.at[:, pl.ds(2 * HEAD, HEAD)]),
        (wkv_ref.at[1], w_all.at[:, pl.ds(4 * HEAD, HEAD)]),
        (wo_ref, wo_all.at[pl.ds(0, HEAD)]),
    ]
    loads = [pltpu.make_async_copy(a, b, load.at[i]) for i, (a, b) in enumerate(loads)]
    for copy in loads:
        copy.start()

    barrier = pltpu.get_barrier_semaphore()
    near = [up, down, mate, other]
    near += [{"section": s, "tower": t} for s in (later, sooner) for t in (tower, 1 - tower)]
    for device in near:
        pl.semaphore_signal(barrier, inc=1, device_id=device, device_id_type=MESH)
    pl.semaphore_wait(barrier, len(near))

    def remote(src, dst, send, recv, device):
        return pltpu.make_async_remote_copy(
            src_ref=src, dst_ref=dst, send_sem=send, recv_sem=recv, device_id=device, device_id_type=MESH
        )

    swaps = [
        remote(x_ref, xp.at[0], in_s.at[2], in_r.at[2], other),
        remote(gain_ref, gains.at[1], in_s.at[3], in_r.at[3], other),
        remote(wq_ref, w_all.at[:, pl.ds(HEAD, HEAD)], w_s.at[0], w_r.at[0], mate),
        remote(wkv_ref.at[0], w_all.at[:, pl.ds(3 * HEAD, HEAD)], w_s.at[1], w_r.at[1], mate),
        remote(wkv_ref.at[1], w_all.at[:, pl.ds(5 * HEAD, HEAD)], w_s.at[2], w_r.at[2], mate),
        remote(wo_ref, wo_all.at[pl.ds(HEAD, HEAD)], w_s.at[3], w_r.at[3], mate),
    ]
    for copy in swaps:
        copy.start()

    first_section = section == 0
    pick = pltpu.make_async_copy(fresh_ref, fresh, load.at[6])

    @pl.when(first_section)
    def _():
        pick.start()

    started = list(swaps)

    def gather(t, which, half, src, dst, device):
        copy = remote(
            rows.at[t, which, half, src],
            rows.at[t, which, half, dst],
            ag_s.at[t, which, half, dst],
            ag_r.at[t, which, half, dst],
            device,
        )
        return copy

    def pass_on(t, which, half, stage):
        copies = []
        if stage < 3 or which == 0:
            copies.append(gather(t, which, half, BACK[stage], BACK[stage + 1], up))
        if stage < 3 or which == 1:
            copies.append(gather(t, which, half, AHEAD[stage], AHEAD[stage + 1], down))
        for copy in copies:
            copy.start()
        started.extend(copies)

    def arrive(t, which, half, slot):
        gather(t, which, half, slot, slot, up).wait_recv()

    def put_normed(t, which, raw):
        value = normed(raw, gains[which])
        for half in range(2):
            rows[t, which, half, 0] = value[:, half * hd : (half + 1) * hd]
            pass_on(t, which, half, 0)

    def project(t, which, stage, first, last):
        lo, hi = STAGES[stage]
        total = None
        for half in range(2):
            block = rows[t, which, half, lo:hi].reshape((hi - lo) * tok, hd)
            term = jnp.dot(block, w_all[half * hd : (half + 1) * hd, first:last], preferred_element_type=F32)
            total = term if total is None else total + term
        return total.astype(BF)

    def attend(stage, query, keyval):
        lo, hi = STAGES[stage]
        m = (hi - lo) * tok
        pieces = []
        for head in range(2):
            q = query[:, head * HEAD : (head + 1) * HEAD]
            k = keyval[:, head * HEAD : (head + 1) * HEAD]
            v = keyval[:, (2 + head) * HEAD : (3 + head) * HEAD]
            scores = lax.dot_general(q, k, (((1,), (1,)), ((), ())), preferred_element_type=F32) * (1 / math.sqrt(HEAD))
            if hi - lo > 1:
                mine = lax.broadcasted_iota(jnp.int32, (m, m), 0) // tok == lax.broadcasted_iota(jnp.int32, (m, m), 1) // tok
                scores = jnp.where(mine, scores, -jnp.inf)
            raised = jnp.exp(scores - jnp.max(scores, -1, keepdims=True))
            weights = (raised / jnp.sum(raised, -1, keepdims=True)).astype(BF)
            pieces.append(jnp.dot(weights, v, preferred_element_type=F32).astype(BF))
        mixed = jnp.concatenate(pieces, axis=1)
        for half in range(2):
            out = jnp.dot(mixed, wo_all[:, half * hd : (half + 1) * hd], preferred_element_type=F32)
            part[half, lo:hi] = out.reshape(hi - lo, tok, hd)

    def reduced(t, way, half, k):
        return remote(
            rsend.at[t, way, half, k - 1],
            rrecv.at[t, way, half, k - 1],
            rs_s.at[t, way, half, k - 1],
            rs_r.at[t, way, half, k - 1],
            down if way == 0 else up,
        )

    def reduce_step(t, way, half, k, opens):
        slot = (BACK if way == 0 else AHEAD)[k]
        value = part[half, slot]
        if not opens:
            reduced(t, way, half, k + 1).wait_recv()
            value = value + rrecv[t, way, half, k].astype(F32)
        rsend[t, way, half, k - 1] = value.astype(BF)
        copy = reduced(t, way, half, k)
        copy.start()
        started.append(copy)

    def reduce_pair(t, k, long):
        for way in range(2):
            half = way if long else 1 - way
            reduce_step(t, way, half, k, k == (4 if long else 3))

    for t in range(2):
        if t == 0:
            loads[0].wait()
            loads[1].wait()
        else:

            @pl.when(section > 0)
            def _():
                remote(outv.at[0], xo.at[1], in_s.at[0], in_r.at[0], up).wait_recv()

        put_normed(t, 0, xo[t])
        if t == 0:
            swaps[0].wait_recv()
            swaps[1].wait_recv()
        else:
            remote(outv.at[0], xp.at[1], in_s.at[1], in_r.at[1], up).wait_recv()
        put_normed(t, 1, xp[t])
        if t == 0:
            for copy in loads[2:]:
                copy.wait()
            for copy in swaps[2:]:
                copy.wait_recv()

            @pl.when(first_section)
            def _():
                pick.wait()
                xo[1] = fresh[off_ref[0]]
                remote(xo.at[1], xp.at[1], in_s.at[1], in_r.at[1], other).start()

        query = project(t, 0, 0, 0, 2 * HEAD)
        attend(0, query, project(t, 1, 0, 2 * HEAD, 6 * HEAD))
        for stage in range(1, 4):
            for half in range(2):
                arrive(t, 0, half, BACK[stage])
                arrive(t, 0, half, AHEAD[stage])
                pass_on(t, 0, half, stage)
            query = project(t, 0, stage, 0, 2 * HEAD)
            for half in range(2):
                arrive(t, 1, half, BACK[stage])
                arrive(t, 1, half, AHEAD[stage])
                pass_on(t, 1, half, stage)
            attend(stage, query, project(t, 1, stage, 2 * HEAD, 6 * HEAD))
        reduce_pair(t, 3, False)
        arrive(t, 0, 0, 7)
        arrive(t, 0, 1, 7)
        query = project(t, 0, 4, 0, 2 * HEAD)
        arrive(t, 1, 0, 7)
        arrive(t, 1, 1, 7)
        attend(4, query, project(t, 1, 4, 2 * HEAD, 6 * HEAD))
        reduce_pair(t, 4, True)
        reduce_pair(t, 2, False)
        reduce_pair(t, 3, True)
        reduce_pair(t, 1, False)
        reduce_pair(t, 2, True)
        reduce_pair(t, 1, True)
        for half in range(2):
            total = part[half, 0]
            for way in range(2):
                reduced(t, way, half, 1).wait_recv()
                total = total + rrecv[t, way, half, 0].astype(F32)
            cols = slice(half * hd, (half + 1) * hd)
            outv[t, :, cols] = (xo[t, :, cols].astype(F32) + total).astype(BF)
        if t == 0:

            @pl.when(section < n_sec - 1)
            def _():
                remote(outv.at[0], xo.at[1], in_s.at[0], in_r.at[0], {"section": later, "tower": tower}).start()
                remote(outv.at[0], xp.at[1], in_s.at[4], in_r.at[1], {"section": later, "tower": 1 - tower}).start()

        pltpu.make_async_copy(outv.at[t], out_ref.at[t], load.at[7 + t]).start()

    for copy in started:
        copy.wait_send()

    @pl.when(first_section)
    def _():
        remote(xo.at[1], xp.at[1], in_s.at[1], in_r.at[1], other).wait_send()

    @pl.when(section < n_sec - 1)
    def _():
        remote(outv.at[0], xo.at[1], in_s.at[0], in_r.at[0], {"section": later, "tower": tower}).wait_send()
        remote(outv.at[0], xp.at[1], in_s.at[4], in_r.at[1], {"section": later, "tower": 1 - tower}).wait_send()

    for t in range(2):
        pltpu.make_async_copy(outv.at[t], out_ref.at[t], load.at[7 + t]).wait()


def shards(n_sec, n_lane, in_flight, fresh_batches, offsets, norm_gain, w_query, w_keyval, w_out):
    tok, d = in_flight.shape[2:]
    anywhere = pl.BlockSpec(memory_space=pl.ANY)
    dma = pltpu.SemaphoreType.DMA
    states = pl.pallas_call(
        functools.partial(kernel, n_sec, n_lane),
        out_shape=jax.ShapeDtypeStruct((2, tok, d), BF),
        in_specs=[anywhere, anywhere, pl.BlockSpec(memory_space=pltpu.SMEM)] + [anywhere] * 4,
        out_specs=anywhere,
        scratch_shapes=[
            pltpu.VMEM((2, tok, d), BF),
            pltpu.VMEM((2, tok, d), BF),
            pltpu.VMEM((2, 1, d), F32),
            pltpu.VMEM((d, 6 * HEAD), BF),
            pltpu.VMEM((2 * HEAD, d), BF),
            pltpu.VMEM((fresh_batches.shape[0], tok, d), BF),
            pltpu.VMEM((2, 2, 2, 8, tok, d // 2), BF),
            pltpu.VMEM((2, 8, tok, d // 2), F32),
            pltpu.VMEM((2, 2, 2, 4, tok, d // 2), BF),
            pltpu.VMEM((2, 2, 2, 4, tok, d // 2), BF),
            pltpu.VMEM((2, tok, d), BF),
            dma((2, 2, 2, 8)),
            dma((2, 2, 2, 8)),
            dma((2, 2, 2, 4)),
            dma((2, 2, 2, 4)),
            dma((5,)),
            dma((5,)),
            dma((4,)),
            dma((4,)),
            dma((9,)),
        ],
        compiler_params=pltpu.CompilerParams(collective_id=0, has_side_effects=True, vmem_limit_bytes=60 * 2**20),
        name="relay",
    )(in_flight[0, 0], fresh_batches[:, 0], offsets, norm_gain[0], w_query[0, 0], w_keyval[0, 0], w_out[0, 0])
    return states[:, None, None]


def solution(mesh):
    placed = (
        P("section", "tower", "lane", None),
        P(None, "tower", "lane", None),
        P("lane"),
        P("section", "tower", None),
        P("section", "tower", None, "lane"),
        P("section", "tower", None, None, "lane"),
        P("section", "tower", "lane", None),
    )
    return jax.shard_map(
        functools.partial(shards, mesh.shape["section"], mesh.shape["lane"]),
        mesh=mesh,
        in_specs=placed,
        out_specs=P(None, "section", "tower", "lane", None),
        check_vma=False,
    )
```

```python
import functools
import math

import jax
import jax.numpy as jnp
from jax import lax
from jax.experimental import pallas as pl
from jax.experimental.pallas import tpu as pltpu
from jax.sharding import PartitionSpec as P

HEAD = 128
EPS = 1e-06
MESH = pl.DeviceIdType.MESH
BF = jnp.bfloat16
F32 = jnp.float32
STAGES = ((0, 1), (1, 3), (3, 5), (5, 7), (7, 8))
BACK = (0, 1, 3, 5, 7)
AHEAD = (0, 2, 4, 6, 7)
PIECES = (0, 2, 1, 3)


def normed(rows, gain):
    wide = rows.astype(F32)
    mean = jnp.mean(wide * wide, -1, keepdims=True)
    return (wide * lax.rsqrt(mean + EPS) * gain).astype(BF)


def kernel(
    n_sec,
    n_lane,
    x_ref,
    fresh_ref,
    off_ref,
    gain_ref,
    wq_ref,
    wkv_ref,
    wo_ref,
    out_ref,
    xo,
    xp,
    gains,
    w_all,
    wo_all,
    fresh,
    rows,
    part,
    rsend,
    rrecv,
    outv,
    picked,
    kv,
    off,
    ready,
    ag_s,
    ag_r,
    rs_s,
    rs_r,
    in_s,
    in_r,
    w_s,
    w_r,
    b_s,
    b_r,
    h_s,
    h_r,
    load,
):
    section = lax.axis_index("section")
    tower = lax.axis_index("tower")
    lane = lax.axis_index("lane")
    d = x_ref.shape[-1]
    hd, qd = d // 2, d // 4
    tok = x_ref.shape[0]
    up = {"lane": lax.rem(lane + 2, n_lane)}
    down = {"lane": lax.rem(lane + n_lane - 2, n_lane)}
    mate_lane = lane + 1 - 2 * lax.rem(lane, 2)
    mate = {"lane": mate_lane}
    other = {"tower": 1 - tower}
    across = {"tower": 1 - tower, "lane": mate_lane}
    later = lax.rem(section + 1, n_sec)
    sooner = lax.rem(section + n_sec - 1, n_sec)

    barrier = pltpu.get_barrier_semaphore()
    near = (up, down, mate, other)
    after = [{"section": later, "tower": t, "lane": mate_lane} for t in (tower, 1 - tower)]
    before = [{"section": sooner, "tower": t, "lane": mate_lane} for t in (tower, 1 - tower)]
    for device in near:
        pl.semaphore_signal(barrier, inc=1, device_id=device, device_id_type=MESH)

    @pl.when(section < n_sec - 1)
    def _():
        for device in after:
            pl.semaphore_signal(barrier, inc=1, device_id=device, device_id_type=MESH)

    loads = [
        (x_ref, xo.at[0]),
        (gain_ref, gains.at[0]),
        (wq_ref, w_all.at[:, pl.ds(0, HEAD)]),
        (wkv_ref.at[0], w_all.at[:, pl.ds(2 * HEAD, HEAD)]),
        (wkv_ref.at[1], w_all.at[:, pl.ds(4 * HEAD, HEAD)]),
        (wo_ref, wo_all.at[pl.ds(0, HEAD)]),
        (off_ref, off),
    ]
    loads = [pltpu.make_async_copy(a, b, load.at[i]) for i, (a, b) in enumerate(loads)]
    for copy in loads:
        copy.start()

    @pl.when(section == 0)
    def _():
        pl.semaphore_signal(barrier, inc=1, device_id=across, device_id_type=MESH)
        pl.semaphore_wait(barrier, len(near) + 1)

    @pl.when(section > 0)
    def _():
        pl.semaphore_wait(barrier, len(near) + 2)
        for device in before:
            pl.semaphore_signal(ready, inc=1, device_id=device, device_id_type=MESH)

    def remote(src, dst, send, recv, device):
        return pltpu.make_async_remote_copy(
            src_ref=src, dst_ref=dst, send_sem=send, recv_sem=recv, device_id=device, device_id_type=MESH
        )

    swaps = [
        remote(x_ref, xp.at[0], in_s.at[0], in_r.at[0], other),
        remote(gain_ref, gains.at[1], in_s.at[1], in_r.at[1], other),
        remote(wq_ref, w_all.at[:, pl.ds(HEAD, HEAD)], w_s.at[0], w_r.at[0], mate),
        remote(wkv_ref.at[0], w_all.at[:, pl.ds(3 * HEAD, HEAD)], w_s.at[1], w_r.at[1], mate),
        remote(wkv_ref.at[1], w_all.at[:, pl.ds(5 * HEAD, HEAD)], w_s.at[2], w_r.at[2], mate),
        remote(wo_ref, wo_all.at[pl.ds(HEAD, HEAD)], w_s.at[3], w_r.at[3], mate),
    ]
    for copy in swaps:
        copy.start()

    first_section = section == 0
    not_first = section > 0
    not_last = section < n_sec - 1
    pick = pltpu.make_async_copy(fresh_ref, fresh, load.at[9])

    @pl.when(first_section)
    def _():
        pick.start()

    started = list(swaps)

    def gather(t, which, half, src, dst, device):
        copy = remote(
            rows.at[t, which, half, src],
            rows.at[t, which, half, dst],
            ag_s.at[t, which, half, dst],
            ag_r.at[t, which, half, dst],
            device,
        )
        return copy

    def routes(stage, which):
        if stage < 3 or which == 0:
            yield BACK[stage], BACK[stage + 1], up
        if stage < 3 or which == 1:
            yield AHEAD[stage], AHEAD[stage + 1], down

    def pass_on(t, which, half, stage):
        for src, dst, device in routes(stage, which):
            gather(t, which, half, src, dst, device).start()

    def gathers_sent(t):
        for which in range(2):
            for half in range(2):
                for stage in range(4):
                    for src, dst, device in routes(stage, which):
                        gather(t, which, half, src, dst, device).wait_send()

    def arrive(t, which, half, slot):
        gather(t, which, half, slot, slot, up).wait_recv()

    def put_normed(t, which, raw):
        value = normed(raw, gains[which])
        for half in range(2):
            rows[t, which, half, 0] = value[:, half * hd : (half + 1) * hd]
            pass_on(t, which, half, 0)

    def partial(t, which, stage, half, first, last):
        lo, hi = STAGES[stage]
        block = rows[t, which, half, lo:hi].reshape((hi - lo) * tok, hd)
        return jnp.dot(block, w_all[half * hd : (half + 1) * hd, first:last], preferred_element_type=F32)

    def work(t, stage):
        held = {}

        def queries():
            held["q"] = (partial(t, 0, stage, 0, 0, 2 * HEAD) + partial(t, 0, stage, 1, 0, 2 * HEAD)).astype(BF)

        def keys_first():
            kv[: (STAGES[stage][1] - STAGES[stage][0]) * tok] = partial(t, 1, stage, 0, 2 * HEAD, 6 * HEAD)

        def keys_last():
            first = kv[: (STAGES[stage][1] - STAGES[stage][0]) * tok]
            held["kv"] = (first + partial(t, 1, stage, 1, 2 * HEAD, 6 * HEAD)).astype(BF)

        def mix(then=None):
            attend(stage, held["q"], held["kv"], then)

        return queries, keys_first, keys_last, mix

    def land(t, which, half, stage):
        if stage < 4:
            arrive(t, which, half, BACK[stage])
            arrive(t, which, half, AHEAD[stage])
            pass_on(t, which, half, stage)
        else:
            arrive(t, which, half, 7)

    def attend(stage, query, keyval, then=None):
        lo, hi = STAGES[stage]
        m = (hi - lo) * tok
        pieces = []
        for head in range(2):
            q = query[:, head * HEAD : (head + 1) * HEAD]
            k = keyval[:, head * HEAD : (head + 1) * HEAD]
            v = keyval[:, (2 + head) * HEAD : (3 + head) * HEAD]
            scores = lax.dot_general(q, k, (((1,), (1,)), ((), ())), preferred_element_type=F32) * (1 / math.sqrt(HEAD))
            if hi - lo > 1:
                mine = lax.broadcasted_iota(jnp.int32, (m, m), 0) // tok == lax.broadcasted_iota(jnp.int32, (m, m), 1) // tok
                scores = jnp.where(mine, scores, -jnp.inf)
            raised = jnp.exp(scores - jnp.max(scores, -1, keepdims=True))
            weights = (raised / jnp.sum(raised, -1, keepdims=True)).astype(BF)
            pieces.append(jnp.dot(weights, v, preferred_element_type=F32).astype(BF))
        mixed = jnp.concatenate(pieces, axis=1)
        for piece in PIECES:
            out = jnp.dot(mixed, wo_all[:, piece * qd : (piece + 1) * qd], preferred_element_type=F32)
            part[piece, lo:hi] = out.reshape(hi - lo, tok, qd)
            if then is not None:
                then(piece)

    def reduced(t, way, half, k):
        return remote(
            rsend.at[t, way, half, k - 1],
            rrecv.at[t, way, half, k - 1],
            rs_s.at[t, way, half, k - 1],
            rs_r.at[t, way, half, k - 1],
            down if way == 0 else up,
        )

    def reduce_step(t, way, half, k, opens):
        slot = (BACK if way == 0 else AHEAD)[k]
        value = part[half, slot]
        if not opens:
            reduced(t, way, half, k + 1).wait_recv()
            value = value + rrecv[t, way, half, k].astype(F32)
        rsend[t, way, half, k - 1] = value.astype(BF)
        copy = reduced(t, way, half, k)
        copy.start()
        started.append(copy)

    def reduce_pair(t, k, long, pieces=PIECES):
        for piece in pieces:
            way = piece // 2 if long else 1 - piece // 2
            reduce_step(t, way, piece, k, k == (4 if long else 3))

    def handed(src, piece, which, device, send):
        cols = pl.ds(piece * qd, qd)
        buffer = (xo, xp)[which]
        return remote(src.at[:, cols], buffer.at[1, :, cols], h_s.at[send, which, piece], h_r.at[which, piece], device)

    def hand_over(piece):
        return [handed(outv.at[0], piece, which, after[which], 0) for which in range(2)]

    def hand_picked(piece):
        return [handed(picked, piece, which, (mate, across)[which], 1) for which in range(2)]

    def back(piece):
        cols = pl.ds(piece * qd, qd)
        return remote(outv.at[1, :, cols], out_ref.at[1, :, cols], b_s.at[piece], b_r.at[piece], mate)

    def enter():
        for which, buffer in enumerate((xo, xp)):
            for piece in PIECES:
                handed(outv.at[0], piece, which, up, 0).wait_recv()
            put_normed(1, which, buffer[1])

    for t in range(2):
        if t == 0:
            loads[0].wait()
            loads[1].wait()
            put_normed(t, 0, xo[t])
            for half in range(2):
                land(t, 0, half, 1)
            swaps[0].wait_recv()
            swaps[1].wait_recv()
            put_normed(t, 1, xp[t])
            for copy in loads[2:]:
                copy.wait()
            for copy in swaps[2:]:
                copy.wait_recv()
            for piece in work(t, 0):
                piece()

            @pl.when(first_section)
            def _():
                pick.wait()
                picked[...] = fresh[off[0]]
                for piece in PIECES:
                    for copy in hand_picked(piece):
                        copy.start()

        else:
            pl.when(not_first)(enter)
        ahead = 1 - t
        for stage in range(1, 4):
            pieces = work(t, stage - 1) if stage > 1 or t == 1 else [None] * 4
            parts = [(0, 0, stage + ahead), (0, 1, stage + ahead), (1, 0, stage), (1, 1, stage)]
            for piece, (which, half, k) in zip(pieces, parts):
                if piece is not None:
                    piece()
                land(t, which, half, k)
        for piece in work(t, 3):
            piece()
        reduce_pair(t, 3, False)
        if t == 1:
            for half in range(2):
                land(t, 0, half, 4)
        queries, keys_first, keys_last, mix = work(t, 4)
        queries()
        land(t, 1, 0, 4)
        keys_first()
        land(t, 1, 1, 4)
        keys_last()
        mix(lambda piece: reduce_pair(t, 4, True, (piece,)))
        reduce_pair(t, 2, False)
        reduce_pair(t, 3, True)
        reduce_pair(t, 1, False)
        reduce_pair(t, 2, True)
        reduce_pair(t, 1, True)
        if t == 0:
            pl.when(first_section)(enter)
            pl.when(not_last)(lambda: pl.semaphore_wait(ready, 2))
        for piece in PIECES:
            total = part[piece, 0]
            for way in (1 - piece // 2, piece // 2):
                reduced(t, way, piece, 1).wait_recv()
                total = total + rrecv[t, way, piece, 0].astype(F32)
            cols = slice(piece * qd, (piece + 1) * qd)
            outv[t, :, cols] = (xo[t, :, cols].astype(F32) + total).astype(BF)
            if t == 1:
                back(piece).start()
            else:

                @pl.when(not_last)
                def _():
                    for copy in hand_over(piece):
                        copy.start()

        if t == 0:
            out_ref[0] = outv[0]
        else:
            gathers_sent(0)
            gathers_sent(1)

    for copy in started:
        copy.wait_send()

    @pl.when(first_section)
    def _():
        for piece in PIECES:
            for copy in hand_picked(piece):
                copy.wait_send()

    @pl.when(not_last)
    def _():
        for piece in PIECES:
            for copy in hand_over(piece):
                copy.wait_send()

    for piece in PIECES:
        back(piece).wait()


def shards(n_sec, n_lane, in_flight, fresh_batches, offsets, norm_gain, w_query, w_keyval, w_out):
    tok, d = in_flight.shape[2:]
    anywhere = pl.BlockSpec(memory_space=pl.ANY)
    dma = pltpu.SemaphoreType.DMA
    states = pl.pallas_call(
        functools.partial(kernel, n_sec, n_lane),
        out_shape=jax.ShapeDtypeStruct((2, tok, d), BF),
        in_specs=[anywhere] * 7,
        out_specs=pl.BlockSpec(memory_space=pltpu.VMEM),
        scratch_shapes=[
            pltpu.VMEM((2, tok, d), BF),
            pltpu.VMEM((2, tok, d), BF),
            pltpu.VMEM((2, 1, d), F32),
            pltpu.VMEM((d, 6 * HEAD), BF),
            pltpu.VMEM((2 * HEAD, d), BF),
            pltpu.VMEM((fresh_batches.shape[0], tok, d), BF),
            pltpu.VMEM((2, 2, 2, 8, tok, d // 2), BF),
            pltpu.VMEM((4, 8, tok, d // 4), F32),
            pltpu.VMEM((2, 2, 4, 4, tok, d // 4), BF),
            pltpu.VMEM((2, 2, 4, 4, tok, d // 4), BF),
            pltpu.VMEM((2, tok, d), BF),
            pltpu.VMEM((tok, d), BF),
            pltpu.VMEM((2 * tok, 4 * HEAD), F32),
            pltpu.SMEM((1,), jnp.int32),
            pltpu.SemaphoreType.REGULAR,
            dma((2, 2, 2, 8)),
            dma((2, 2, 2, 8)),
            dma((2, 2, 4, 4)),
            dma((2, 2, 4, 4)),
            dma((2,)),
            dma((2,)),
            dma((4,)),
            dma((4,)),
            dma((4,)),
            dma((4,)),
            dma((2, 2, 4)),
            dma((2, 4)),
            dma((10,)),
        ],
        compiler_params=pltpu.CompilerParams(collective_id=0, has_side_effects=True, vmem_limit_bytes=60 * 2**20),
        name="relay",
    )(in_flight[0, 0], fresh_batches[:, 0], offsets, norm_gain[0], w_query[0, 0], w_keyval[0, 0], w_out[0, 0])
    return states[:, None, None]


def solution(mesh):
    placed = (
        P("section", "tower", "lane", None),
        P(None, "tower", "lane", None),
        P("lane"),
        P("section", "tower", None),
        P("section", "tower", None, "lane"),
        P("section", "tower", None, None, "lane"),
        P("section", "tower", "lane", None),
    )
    return jax.shard_map(
        functools.partial(shards, mesh.shape["section"], mesh.shape["lane"]),
        mesh=mesh,
        in_specs=placed,
        out_specs=P(None, "section", "tower", "lane", None),
        check_vma=False,
    )
```

```python
import functools
import math

import jax
import jax.numpy as jnp
from jax import lax
from jax.experimental import pallas as pl
from jax.experimental.pallas import tpu as pltpu
from jax.sharding import PartitionSpec as P

HEAD = 128
EPS = 1e-06
MESH = pl.DeviceIdType.MESH
BF = jnp.bfloat16
F32 = jnp.float32
STAGES = ((0, 1), (1, 3), (3, 5), (5, 7), (7, 8))
BACK = (0, 1, 3, 5, 7)
AHEAD = (0, 2, 4, 6, 7)
PIECES = (0, 2, 1, 3)


def normed(rows, gain):
    wide = rows.astype(F32)
    mean = jnp.mean(wide * wide, -1, keepdims=True)
    return (wide * lax.rsqrt(mean + EPS) * gain).astype(BF)


def kernel(
    n_sec,
    n_lane,
    x_ref,
    fresh_ref,
    off_ref,
    gain_ref,
    wq_ref,
    wkv_ref,
    wo_ref,
    out_ref,
    xo,
    xp,
    gains,
    w_all,
    wo_all,
    fresh,
    rows,
    part,
    rsend,
    rrecv,
    outv,
    picked,
    kv,
    off,
    ready,
    ag_s,
    ag_r,
    rs_s,
    rs_r,
    in_s,
    in_r,
    w_s,
    w_r,
    b_s,
    b_r,
    h_s,
    h_r,
    load,
):
    section = lax.axis_index("section")
    tower = lax.axis_index("tower")
    lane = lax.axis_index("lane")
    d = x_ref.shape[-1]
    hd, qd = d // 2, d // 4
    tok = x_ref.shape[0]
    up = {"lane": lax.rem(lane + 2, n_lane)}
    down = {"lane": lax.rem(lane + n_lane - 2, n_lane)}
    mate_lane = lane + 1 - 2 * lax.rem(lane, 2)
    mate = {"lane": mate_lane}
    other = {"tower": 1 - tower}
    across = {"tower": 1 - tower, "lane": mate_lane}
    later = lax.rem(section + 1, n_sec)
    sooner = lax.rem(section + n_sec - 1, n_sec)

    barrier = pltpu.get_barrier_semaphore()
    near = (up, down, mate, other)
    after = [{"section": later, "tower": t, "lane": mate_lane} for t in (tower, 1 - tower)]
    before = [{"section": sooner, "tower": t, "lane": mate_lane} for t in (tower, 1 - tower)]
    for device in near:
        pl.semaphore_signal(barrier, inc=1, device_id=device, device_id_type=MESH)

    @pl.when(section < n_sec - 1)
    def _():
        for device in after:
            pl.semaphore_signal(barrier, inc=1, device_id=device, device_id_type=MESH)

    loads = [
        (x_ref, xo.at[0]),
        (gain_ref, gains.at[0]),
        (wq_ref, w_all.at[:, pl.ds(0, HEAD)]),
        (wkv_ref.at[0], w_all.at[:, pl.ds(2 * HEAD, HEAD)]),
        (wkv_ref.at[1], w_all.at[:, pl.ds(4 * HEAD, HEAD)]),
        (wo_ref, wo_all.at[pl.ds(0, HEAD)]),
        (off_ref, off),
    ]
    loads = [pltpu.make_async_copy(a, b, load.at[i]) for i, (a, b) in enumerate(loads)]
    for copy in loads:
        copy.start()

    @pl.when(section == 0)
    def _():
        pl.semaphore_signal(barrier, inc=1, device_id=across, device_id_type=MESH)
        pl.semaphore_wait(barrier, len(near) + 1)

    @pl.when(section > 0)
    def _():
        pl.semaphore_wait(barrier, len(near) + 2)
        for device in before:
            pl.semaphore_signal(ready, inc=1, device_id=device, device_id_type=MESH)

    def remote(src, dst, send, recv, device):
        return pltpu.make_async_remote_copy(
            src_ref=src, dst_ref=dst, send_sem=send, recv_sem=recv, device_id=device, device_id_type=MESH
        )

    swaps = [
        remote(x_ref, xp.at[0], in_s.at[0], in_r.at[0], other),
        remote(gain_ref, gains.at[1], in_s.at[1], in_r.at[1], other),
        remote(wq_ref, w_all.at[:, pl.ds(HEAD, HEAD)], w_s.at[0], w_r.at[0], mate),
        remote(wkv_ref.at[0], w_all.at[:, pl.ds(3 * HEAD, HEAD)], w_s.at[1], w_r.at[1], mate),
        remote(wkv_ref.at[1], w_all.at[:, pl.ds(5 * HEAD, HEAD)], w_s.at[2], w_r.at[2], mate),
        remote(wo_ref, wo_all.at[pl.ds(HEAD, HEAD)], w_s.at[3], w_r.at[3], mate),
    ]
    for copy in swaps:
        copy.start()

    first_section = section == 0
    not_first = section > 0
    not_last = section < n_sec - 1
    pick = pltpu.make_async_copy(fresh_ref, fresh, load.at[7])

    @pl.when(first_section)
    def _():
        pick.start()

    started = list(swaps)

    def gather(t, which, half, src, dst, device):
        copy = remote(
            rows.at[t, which, half, src],
            rows.at[t, which, half, dst],
            ag_s.at[t],
            ag_r.at[which, half, dst - 1],
            device,
        )
        return copy

    def routes(stage, which):
        if stage < 3 or which == 0:
            yield BACK[stage], BACK[stage + 1], up
        if stage < 3 or which == 1:
            yield AHEAD[stage], AHEAD[stage + 1], down

    def pass_on(t, which, half, stage):
        for src, dst, device in routes(stage, which):
            gather(t, which, half, src, dst, device).start()

    def sent(ref, sem):
        remote(ref, ref, sem, sem, up).wait_send()

    def arrive(t, which, half, slot):
        gather(t, which, half, slot, slot, up).wait_recv()

    def put_normed(t, which, raw):
        value = normed(raw, gains[which])
        for half in range(2):
            rows[t, which, half, 0] = value[:, half * hd : (half + 1) * hd]
            pass_on(t, which, half, 0)

    def partial(t, which, stage, half, first, last):
        lo, hi = STAGES[stage]
        block = rows[t, which, half, lo:hi].reshape((hi - lo) * tok, hd)
        return jnp.dot(block, w_all[half * hd : (half + 1) * hd, first:last], preferred_element_type=F32)

    def work(t, stage):
        held = {}

        def queries():
            held["q"] = (partial(t, 0, stage, 0, 0, 2 * HEAD) + partial(t, 0, stage, 1, 0, 2 * HEAD)).astype(BF)

        def keys_first():
            kv[: (STAGES[stage][1] - STAGES[stage][0]) * tok] = partial(t, 1, stage, 0, 2 * HEAD, 6 * HEAD)

        def keys_last():
            first = kv[: (STAGES[stage][1] - STAGES[stage][0]) * tok]
            held["kv"] = (first + partial(t, 1, stage, 1, 2 * HEAD, 6 * HEAD)).astype(BF)

        def mix(then=None):
            attend(stage, held["q"], held["kv"], then)

        return queries, keys_first, keys_last, mix

    def land(t, which, half, stage):
        if stage < 4:
            for near_side in (BACK, AHEAD):
                arrive(t, which, half, near_side[stage])
                for link in routes(stage, which):
                    if link[0] == near_side[stage]:
                        gather(t, which, half, *link).start()
        else:
            arrive(t, which, half, 7)

    def attend(stage, query, keyval, then=None):
        lo, hi = STAGES[stage]
        m = (hi - lo) * tok
        pieces = []
        for head in range(2):
            q = query[:, head * HEAD : (head + 1) * HEAD]
            k = keyval[:, head * HEAD : (head + 1) * HEAD]
            v = keyval[:, (2 + head) * HEAD : (3 + head) * HEAD]
            scores = lax.dot_general(q, k, (((1,), (1,)), ((), ())), preferred_element_type=F32) * (1 / math.sqrt(HEAD))
            if hi - lo > 1:
                mine = lax.broadcasted_iota(jnp.int32, (m, m), 0) // tok == lax.broadcasted_iota(jnp.int32, (m, m), 1) // tok
                scores = jnp.where(mine, scores, -jnp.inf)
            raised = jnp.exp(scores - jnp.max(scores, -1, keepdims=True))
            weights = (raised / jnp.sum(raised, -1, keepdims=True)).astype(BF)
            pieces.append(jnp.dot(weights, v, preferred_element_type=F32).astype(BF))
        mixed = jnp.concatenate(pieces, axis=1)
        for piece in PIECES:
            out = jnp.dot(mixed, wo_all[:, piece * qd : (piece + 1) * qd], preferred_element_type=F32)
            part[piece, lo:hi] = out.reshape(hi - lo, tok, qd)
            if then is not None:
                then(piece)

    def reduced(t, way, half, k):
        return remote(
            rsend.at[t, way, half, k - 1],
            rrecv.at[t, way, half, k - 1],
            rs_s.at[t, k // 4],
            rs_r.at[way, half, k - 1],
            down if way == 0 else up,
        )

    def reduce_step(t, way, half, k, opens):
        slot = (BACK if way == 0 else AHEAD)[k]
        value = part[half, slot]
        if not opens:
            reduced(t, way, half, k + 1).wait_recv()
            value = value + rrecv[t, way, half, k].astype(F32)
        rsend[t, way, half, k - 1] = value.astype(BF)
        reduced(t, way, half, k).start()

    def reduce_pair(t, k, long, pieces=PIECES):
        for piece in pieces:
            way = piece // 2 if long else 1 - piece // 2
            reduce_step(t, way, piece, k, k == (4 if long else 3))

    def handed(src, piece, which, device, send):
        cols = pl.ds(piece * qd, qd)
        buffer = (xo, xp)[which]
        return remote(src.at[:, cols], buffer.at[1, :, cols], h_s.at[send, which], h_r.at[which], device)

    def hand_over(piece):
        return [handed(outv.at[0], piece, which, after[which], 0) for which in range(2)]

    def hand_picked(piece):
        return [handed(picked, piece, which, (mate, across)[which], 1) for which in range(2)]

    def back(piece):
        cols = pl.ds(piece * qd, qd)
        return remote(outv.at[1, :, cols], out_ref.at[1, :, cols], b_s, b_r, mate)

    def enter():
        for which, buffer in enumerate((xo, xp)):
            remote(outv.at[0], buffer.at[1], h_s.at[0, which], h_r.at[which], up).wait_recv()
            put_normed(1, which, buffer[1])

    for t in range(2):
        if t == 0:
            loads[0].wait()
            loads[1].wait()
            put_normed(t, 0, xo[t])
            for half in range(2):
                land(t, 0, half, 1)
            swaps[0].wait_recv()
            swaps[1].wait_recv()
            put_normed(t, 1, xp[t])
            for copy in loads[2:]:
                copy.wait()
            for copy in swaps[2:]:
                copy.wait_recv()
            for piece in work(t, 0):
                piece()

            @pl.when(first_section)
            def _():
                pick.wait()
                picked[...] = fresh[off[0]]
                for piece in PIECES:
                    for copy in hand_picked(piece):
                        copy.start()

        else:
            pl.when(not_first)(enter)
        ahead = 1 - t
        for stage in range(1, 4):
            pieces = work(t, stage - 1) if stage > 1 or t == 1 else [None] * 4
            parts = [(0, 0, stage + ahead), (0, 1, stage + ahead), (1, 0, stage), (1, 1, stage)]
            for piece, (which, half, k) in zip(pieces, parts):
                if piece is not None:
                    piece()
                land(t, which, half, k)
        for piece in work(t, 3):
            piece()
        reduce_pair(t, 3, False)
        if t == 1:
            for half in range(2):
                land(t, 0, half, 4)
        queries, keys_first, keys_last, mix = work(t, 4)
        queries()
        land(t, 1, 0, 4)
        keys_first()
        land(t, 1, 1, 4)
        keys_last()
        mix(lambda piece: reduce_pair(t, 4, True, (piece,)))
        reduce_pair(t, 2, False)
        reduce_pair(t, 3, True)
        reduce_pair(t, 1, False)
        reduce_pair(t, 2, True)
        reduce_pair(t, 1, True)
        if t == 0:
            pl.when(first_section)(enter)
            pl.when(not_last)(lambda: pl.semaphore_wait(ready, 2))
        for piece in PIECES:
            total = part[piece, 0]
            for way in (1 - piece // 2, piece // 2):
                reduced(t, way, piece, 1).wait_recv()
                total = total + rrecv[t, way, piece, 0].astype(F32)
            cols = slice(piece * qd, (piece + 1) * qd)
            outv[t, :, cols] = (xo[t, :, cols].astype(F32) + total).astype(BF)
            if t == 1:
                back(piece).start()
            else:

                @pl.when(not_last)
                def _():
                    for copy in hand_over(piece):
                        copy.start()

        if t == 0:
            out_ref[0] = outv[0]
    for copy in started:
        copy.wait_send()

    @pl.when(first_section)
    def _():
        for which in range(2):
            sent(picked, h_s.at[1, which])

    @pl.when(not_last)
    def _():
        for which in range(2):
            sent(outv.at[0], h_s.at[0, which])

    for t in range(2):
        sent(rows.at[t, :, :, 0:7], ag_s.at[t])
        sent(rsend.at[t, :, :, 0:3], rs_s.at[t, 0])
        sent(rsend.at[t, 0, :, 3], rs_s.at[t, 1])
    remote(outv.at[1], out_ref.at[1], b_s, b_r, mate).wait()


def shards(n_sec, n_lane, in_flight, fresh_batches, offsets, norm_gain, w_query, w_keyval, w_out):
    tok, d = in_flight.shape[2:]
    anywhere = pl.BlockSpec(memory_space=pl.ANY)
    dma = pltpu.SemaphoreType.DMA
    states = pl.pallas_call(
        functools.partial(kernel, n_sec, n_lane),
        out_shape=jax.ShapeDtypeStruct((2, tok, d), BF),
        in_specs=[anywhere] * 7,
        out_specs=pl.BlockSpec(memory_space=pltpu.VMEM),
        scratch_shapes=[
            pltpu.VMEM((2, tok, d), BF),
            pltpu.VMEM((2, tok, d), BF),
            pltpu.VMEM((2, 1, d), F32),
            pltpu.VMEM((d, 6 * HEAD), BF),
            pltpu.VMEM((2 * HEAD, d), BF),
            pltpu.VMEM((fresh_batches.shape[0], tok, d), BF),
            pltpu.VMEM((2, 2, 2, 8, tok, d // 2), BF),
            pltpu.VMEM((4, 8, tok, d // 4), F32),
            pltpu.VMEM((2, 2, 4, 4, tok, d // 4), BF),
            pltpu.VMEM((2, 2, 4, 4, tok, d // 4), BF),
            pltpu.VMEM((2, tok, d), BF),
            pltpu.VMEM((tok, d), BF),
            pltpu.VMEM((2 * tok, 4 * HEAD), F32),
            pltpu.SMEM((1,), jnp.int32),
            pltpu.SemaphoreType.REGULAR,
            dma((2,)),
            dma((2, 2, 7)),
            dma((2, 2)),
            dma((2, 4, 4)),
            dma((2,)),
            dma((2,)),
            dma((4,)),
            dma((4,)),
            dma(()),
            dma(()),
            dma((2, 2)),
            dma((2,)),
            dma((8,)),
        ],
        compiler_params=pltpu.CompilerParams(collective_id=0, has_side_effects=True, vmem_limit_bytes=60 * 2**20),
        name="relay",
    )(in_flight[0, 0], fresh_batches[:, 0], offsets, norm_gain[0], w_query[0, 0], w_keyval[0, 0], w_out[0, 0])
    return states[:, None, None]


def solution(mesh):
    placed = (
        P("section", "tower", "lane", None),
        P(None, "tower", "lane", None),
        P("lane"),
        P("section", "tower", None),
        P("section", "tower", None, "lane"),
        P("section", "tower", None, None, "lane"),
        P("section", "tower", "lane", None),
    )
    return jax.shard_map(
        functools.partial(shards, mesh.shape["section"], mesh.shape["lane"]),
        mesh=mesh,
        in_specs=placed,
        out_specs=P(None, "section", "tower", "lane", None),
        check_vma=False,
    )
```

```python
import functools
import math

import jax
import jax.numpy as jnp
from jax import lax
from jax.experimental import pallas as pl
from jax.experimental.pallas import tpu as pltpu
from jax.sharding import PartitionSpec as P

HEAD = 128
EPS = 1e-06
MESH = pl.DeviceIdType.MESH
BF = jnp.bfloat16
F32 = jnp.float32
STAGES = ((0, 1), (1, 3), (3, 5), (5, 7), (7, 8))
BACK = (0, 1, 3, 5, 7)
AHEAD = (0, 2, 4, 6, 7)
PIECES = (0, 2, 1, 3)


def normed(rows, gain):
    wide = rows.astype(F32)
    mean = jnp.mean(wide * wide, -1, keepdims=True)
    return (wide * lax.rsqrt(mean + EPS) * gain).astype(BF)


def kernel(
    n_sec,
    n_lane,
    x_ref,
    fresh_ref,
    off_ref,
    gain_ref,
    wq_ref,
    wkv_ref,
    wo_ref,
    out_ref,
    xo,
    xp,
    gains,
    w_all,
    wo_all,
    fresh,
    rows,
    part,
    rsend,
    rrecv,
    outv,
    picked,
    kv,
    off,
    ready,
    ag_s,
    ag_r,
    rs_s,
    rs_r,
    in_s,
    in_r,
    w_s,
    w_r,
    b_s,
    b_r,
    h_s,
    h_r,
    load,
):
    section = lax.axis_index("section")
    tower = lax.axis_index("tower")
    lane = lax.axis_index("lane")
    d = x_ref.shape[-1]
    hd, qd = d // 2, d // 4
    tok = x_ref.shape[0]
    up = {"lane": lax.rem(lane + 2, n_lane)}
    down = {"lane": lax.rem(lane + n_lane - 2, n_lane)}
    mate_lane = lane + 1 - 2 * lax.rem(lane, 2)
    mate = {"lane": mate_lane}
    other = {"tower": 1 - tower}
    across = {"tower": 1 - tower, "lane": mate_lane}
    later = lax.rem(section + 1, n_sec)
    sooner = lax.rem(section + n_sec - 1, n_sec)

    barrier = pltpu.get_barrier_semaphore()
    near = (up, down, mate, other)
    after = [{"section": later, "tower": t, "lane": mate_lane} for t in (tower, 1 - tower)]
    before = [{"section": sooner, "tower": t, "lane": mate_lane} for t in (tower, 1 - tower)]
    for device in near:
        pl.semaphore_signal(barrier, inc=1, device_id=device, device_id_type=MESH)

    @pl.when(section < n_sec - 1)
    def _():
        for device in after:
            pl.semaphore_signal(barrier, inc=1, device_id=device, device_id_type=MESH)

    loads = [
        (x_ref, xo.at[0]),
        (gain_ref, gains.at[0]),
        (wq_ref, w_all.at[:, pl.ds(0, HEAD)]),
        (wkv_ref.at[0], w_all.at[:, pl.ds(2 * HEAD, HEAD)]),
        (wkv_ref.at[1], w_all.at[:, pl.ds(4 * HEAD, HEAD)]),
        (wo_ref, wo_all.at[pl.ds(0, HEAD)]),
        (off_ref, off),
    ]
    loads = [pltpu.make_async_copy(a, b, load.at[i]) for i, (a, b) in enumerate(loads)]
    for copy in loads:
        copy.start()

    @pl.when(section == 0)
    def _():
        pl.semaphore_signal(barrier, inc=1, device_id=across, device_id_type=MESH)
        pl.semaphore_wait(barrier, len(near) + 1)

    @pl.when(section > 0)
    def _():
        pl.semaphore_wait(barrier, len(near) + 2)
        for device in before:
            pl.semaphore_signal(ready, inc=1, device_id=device, device_id_type=MESH)

    def remote(src, dst, send, recv, device):
        return pltpu.make_async_remote_copy(
            src_ref=src, dst_ref=dst, send_sem=send, recv_sem=recv, device_id=device, device_id_type=MESH
        )

    swaps = [
        remote(x_ref, xp.at[0], in_s.at[0], in_r.at[0], other),
        remote(gain_ref, gains.at[1], in_s.at[1], in_r.at[1], other),
        remote(wq_ref, w_all.at[:, pl.ds(HEAD, HEAD)], w_s.at[0], w_r.at[0], mate),
        remote(wkv_ref.at[0], w_all.at[:, pl.ds(3 * HEAD, HEAD)], w_s.at[1], w_r.at[1], mate),
        remote(wkv_ref.at[1], w_all.at[:, pl.ds(5 * HEAD, HEAD)], w_s.at[2], w_r.at[2], mate),
        remote(wo_ref, wo_all.at[pl.ds(HEAD, HEAD)], w_s.at[3], w_r.at[3], mate),
    ]
    for copy in swaps:
        copy.start()

    first_section = section == 0
    not_first = section > 0
    not_last = section < n_sec - 1
    pick = pltpu.make_async_copy(fresh_ref, fresh, load.at[7])

    @pl.when(first_section)
    def _():
        pick.start()

    started = list(swaps)

    def gather(t, which, half, src, dst, device):
        copy = remote(
            rows.at[t, which, half, src],
            rows.at[t, which, half, dst],
            ag_s.at[t],
            ag_r.at[which, half, dst - 1],
            device,
        )
        return copy

    def routes(stage, which):
        if stage < 3 or which == 0:
            yield BACK[stage], BACK[stage + 1], up
        if stage < 3 or which == 1:
            yield AHEAD[stage], AHEAD[stage + 1], down

    def pass_on(t, which, half, stage):
        for src, dst, device in routes(stage, which):
            gather(t, which, half, src, dst, device).start()

    def sent(ref, sem):
        remote(ref, ref, sem, sem, up).wait_send()

    def arrive(t, which, half, slot):
        gather(t, which, half, slot, slot, up).wait_recv()

    def put_normed(t, which, raw):
        value = normed(raw, gains[which])
        for half in range(2):
            rows[t, which, half, 0] = value[:, half * hd : (half + 1) * hd]
            pass_on(t, which, half, 0)

    def partial(t, which, stage, half, first, last):
        lo, hi = STAGES[stage]
        block = rows[t, which, half, lo:hi].reshape((hi - lo) * tok, hd)
        return jnp.dot(block, w_all[half * hd : (half + 1) * hd, first:last], preferred_element_type=F32)

    def work(t, stage):
        held = {}

        def queries():
            held["q"] = (partial(t, 0, stage, 0, 0, 2 * HEAD) + partial(t, 0, stage, 1, 0, 2 * HEAD)).astype(BF)

        def keys_first():
            kv[: (STAGES[stage][1] - STAGES[stage][0]) * tok] = partial(t, 1, stage, 0, 2 * HEAD, 6 * HEAD)

        def keys_last():
            first = kv[: (STAGES[stage][1] - STAGES[stage][0]) * tok]
            held["kv"] = (first + partial(t, 1, stage, 1, 2 * HEAD, 6 * HEAD)).astype(BF)

        def mix(then=None):
            attend(stage, held["q"], held["kv"], then)

        return queries, keys_first, keys_last, mix

    def land(t, which, half, stage):
        if stage < 4:
            for near_side in (BACK, AHEAD):
                arrive(t, which, half, near_side[stage])
                for link in routes(stage, which):
                    if link[0] == near_side[stage]:
                        gather(t, which, half, *link).start()
        else:
            arrive(t, which, half, 7)

    def attend(stage, query, keyval, then=None):
        lo, hi = STAGES[stage]
        m = (hi - lo) * tok
        pieces = []
        for head in range(2):
            q = query[:, head * HEAD : (head + 1) * HEAD]
            k = keyval[:, head * HEAD : (head + 1) * HEAD]
            v = keyval[:, (2 + head) * HEAD : (3 + head) * HEAD]
            scores = lax.dot_general(q, k, (((1,), (1,)), ((), ())), preferred_element_type=F32) * (1 / math.sqrt(HEAD))
            if hi - lo > 1:
                mine = lax.broadcasted_iota(jnp.int32, (m, m), 0) // tok == lax.broadcasted_iota(jnp.int32, (m, m), 1) // tok
                scores = jnp.where(mine, scores, -jnp.inf)
            raised = jnp.exp(scores - jnp.max(scores, -1, keepdims=True))
            weights = (raised / jnp.sum(raised, -1, keepdims=True)).astype(BF)
            pieces.append(jnp.dot(weights, v, preferred_element_type=F32).astype(BF))
        mixed = jnp.concatenate(pieces, axis=1)
        for piece in PIECES:
            out = jnp.dot(mixed, wo_all[:, piece * qd : (piece + 1) * qd], preferred_element_type=F32)
            part[piece, lo:hi] = out.reshape(hi - lo, tok, qd)
            if then is not None:
                then(piece)

    def reduced(t, way, half, k):
        return remote(
            rsend.at[t, way, half, k - 1],
            rrecv.at[t, way, half, k - 1],
            rs_s.at[t, k // 4],
            rs_r.at[way, half, k - 1],
            down if way == 0 else up,
        )

    def reduce_step(t, way, half, k, opens):
        slot = (BACK if way == 0 else AHEAD)[k]
        value = part[half, slot]
        if not opens:
            reduced(t, way, half, k + 1).wait_recv()
            value = value + rrecv[t, way, half, k].astype(F32)
        rsend[t, way, half, k - 1] = value.astype(BF)
        reduced(t, way, half, k).start()

    def reduce_pair(t, k, long, pieces=PIECES):
        for piece in pieces:
            way = piece // 2 if long else 1 - piece // 2
            reduce_step(t, way, piece, k, k == (4 if long else 3))

    def handed(src, piece, which, device, send):
        cols = pl.ds(piece * qd, qd)
        buffer = (xo, xp)[which]
        return remote(src.at[:, cols], buffer.at[1, :, cols], h_s.at[send, which], h_r.at[which], device)

    def hand_over(piece):
        return [handed(outv.at[0], piece, which, after[which], 0) for which in range(2)]

    def hand_picked(piece):
        return [handed(picked, piece, which, (mate, across)[which], 1) for which in range(2)]

    def back(piece):
        cols = pl.ds(piece * qd, qd)
        return remote(outv.at[1, :, cols], out_ref.at[1, :, cols], b_s, b_r, mate)

    def enter():
        for which, buffer in enumerate((xo, xp)):
            remote(outv.at[0], buffer.at[1], h_s.at[0, which], h_r.at[which], up).wait_recv()
            put_normed(1, which, buffer[1])

    for t in range(2):
        if t == 0:
            loads[0].wait()
            loads[1].wait()
            put_normed(t, 0, xo[t])
            for half in range(2):
                land(t, 0, half, 1)
            swaps[0].wait_recv()
            swaps[1].wait_recv()
            put_normed(t, 1, xp[t])
            for copy in loads[2:]:
                copy.wait()
            for copy in swaps[2:]:
                copy.wait_recv()
            for piece in work(t, 0):
                piece()

            @pl.when(first_section)
            def _():
                pick.wait()
                picked[...] = fresh[off[0]]
                for piece in PIECES:
                    for copy in hand_picked(piece):
                        copy.start()

        else:
            pl.when(not_first)(enter)
        ahead = 1 - t
        for stage in range(1, 4):
            pieces = work(t, stage - 1) if stage > 1 or t == 1 else [None] * 4
            parts = [(0, 0, stage + ahead), (0, 1, stage + ahead), (1, 0, stage), (1, 1, stage)]
            for piece, (which, half, k) in zip(pieces, parts):
                if piece is not None:
                    piece()
                land(t, which, half, k)
        for piece in work(t, 3):
            piece()
        reduce_pair(t, 3, False)
        if t == 1:
            for half in range(2):
                land(t, 0, half, 4)
        queries, keys_first, keys_last, mix = work(t, 4)
        queries()
        land(t, 1, 0, 4)
        keys_first()
        land(t, 1, 1, 4)
        keys_last()
        mix(lambda piece: reduce_pair(t, 4, True, (piece,)))
        reduce_pair(t, 2, False)
        reduce_pair(t, 3, True)
        reduce_pair(t, 1, False)
        reduce_pair(t, 2, True)
        reduce_pair(t, 1, True)
        if t == 0:
            pl.when(first_section)(enter)
            pl.when(not_last)(lambda: pl.semaphore_wait(ready, 2))
        for piece in PIECES:
            total = part[piece, 0]
            for way in (1 - piece // 2, piece // 2):
                reduced(t, way, piece, 1).wait_recv()
                total = total + rrecv[t, way, piece, 0].astype(F32)
            cols = slice(piece * qd, (piece + 1) * qd)
            outv[t, :, cols] = (xo[t, :, cols].astype(F32) + total).astype(BF)
            if t == 1:
                back(piece).start()
            else:

                @pl.when(not_last)
                def _():
                    for copy in hand_over(piece):
                        copy.start()

        if t == 0:
            keep = pltpu.make_async_copy(outv.at[0], out_ref.at[0], load.at[0])
            keep.start()

    for copy in started:
        copy.wait_send()

    @pl.when(first_section)
    def _():
        for which in range(2):
            sent(picked, h_s.at[1, which])

    @pl.when(not_last)
    def _():
        for which in range(2):
            sent(outv.at[0], h_s.at[0, which])

    for t in range(2):
        sent(rows.at[t, :, :, 0:7], ag_s.at[t])
        sent(rsend.at[t, :, :, 0:3], rs_s.at[t, 0])
        sent(rsend.at[t, 0, :, 3], rs_s.at[t, 1])
    keep.wait()
    remote(outv.at[1], out_ref.at[1], b_s, b_r, mate).wait()


def shards(n_sec, n_lane, in_flight, fresh_batches, offsets, norm_gain, w_query, w_keyval, w_out):
    tok, d = in_flight.shape[2:]
    anywhere = pl.BlockSpec(memory_space=pl.ANY)
    dma = pltpu.SemaphoreType.DMA
    states = pl.pallas_call(
        functools.partial(kernel, n_sec, n_lane),
        out_shape=jax.ShapeDtypeStruct((2, tok, d), BF),
        in_specs=[anywhere] * 7,
        out_specs=anywhere,
        scratch_shapes=[
            pltpu.VMEM((2, tok, d), BF),
            pltpu.VMEM((2, tok, d), BF),
            pltpu.VMEM((2, 1, d), F32),
            pltpu.VMEM((d, 6 * HEAD), BF),
            pltpu.VMEM((2 * HEAD, d), BF),
            pltpu.VMEM((fresh_batches.shape[0], tok, d), BF),
            pltpu.VMEM((2, 2, 2, 8, tok, d // 2), BF),
            pltpu.VMEM((4, 8, tok, d // 4), F32),
            pltpu.VMEM((2, 2, 4, 4, tok, d // 4), BF),
            pltpu.VMEM((2, 2, 4, 4, tok, d // 4), BF),
            pltpu.VMEM((2, tok, d), BF),
            pltpu.VMEM((tok, d), BF),
            pltpu.VMEM((2 * tok, 4 * HEAD), F32),
            pltpu.SMEM((1,), jnp.int32),
            pltpu.SemaphoreType.REGULAR,
            dma((2,)),
            dma((2, 2, 7)),
            dma((2, 2)),
            dma((2, 4, 4)),
            dma((2,)),
            dma((2,)),
            dma((4,)),
            dma((4,)),
            dma(()),
            dma(()),
            dma((2, 2)),
            dma((2,)),
            dma((8,)),
        ],
        compiler_params=pltpu.CompilerParams(collective_id=0, has_side_effects=True, vmem_limit_bytes=60 * 2**20),
        name="relay",
    )(in_flight[0, 0], fresh_batches[:, 0], offsets, norm_gain[0], w_query[0, 0], w_keyval[0, 0], w_out[0, 0])
    return states[:, None, None]


def solution(mesh):
    placed = (
        P("section", "tower", "lane", None),
        P(None, "tower", "lane", None),
        P("lane"),
        P("section", "tower", None),
        P("section", "tower", None, "lane"),
        P("section", "tower", None, None, "lane"),
        P("section", "tower", "lane", None),
    )
    return jax.shard_map(
        functools.partial(shards, mesh.shape["section"], mesh.shape["lane"]),
        mesh=mesh,
        in_specs=placed,
        out_specs=P(None, "section", "tower", "lane", None),
        check_vma=False,
    )
```
